512 devices in a mesh: dap: 128 (over x_hi, y, z), grp: 4 (over x_lo, core).
Axes of the slice: x: 4 (x_hi: 2, x_lo: 2; x = x_hi * 2 + x_lo), y: 4, z: 16, core: 2. Of those that a mesh axis runs over, the one named last changes fastest.
Arguments:
- pair_rep: bfloat16 [1024, 1024, 128], P('dap', 'grp'), may hold values from -6 to 6
- chain_ids: int32 [1024], replicated, may hold values from 0 to 7, never falling along the last dimension, each value on 1 to 256 neighbouring positions
- crop_lengths: int32 [8], replicated, may hold values from 64 to 256
- ln_in_gain: float32 [2, 128], replicated, may hold values from 0.1 to 1.9
- w_proj: bfloat16 [2, 128, 512], replicated, may hold values from -0.5 to 0.5
- w_gate: bfloat16 [2, 128, 128], replicated, may hold values from -0.5 to 0.5
- ln_out_gain: float32 [2, 128], replicated, may hold values from 0.1 to 1.9
- w_out: bfloat16 [2, 128, 128], replicated, may hold values from -0.5 to 0.5
Outputs:
- pair_out: bfloat16 [1024, 1024, 128], P('dap', 'grp')
The draws below stay inside these ranges and needn't reach their ends.
Inputs may be any that keep to these rules, and one draw needn't show every extreme that they name: `chain_ids`: chain ids never fall along the residues; each chain holds 1 to 256 residues, and some chain exactly 256.
All inputs are finite; a program needn't handle non-finite values.
Results may differ from the reference program's by a relative error of at most 0.0095.
Values may be sent and summed in bfloat16 or wider, within the bound.
A program may use at most 64 MiB of HBM per device.

```python
import math
import jax
import jax.numpy as jnp
import numpy as np
from jax import lax

D = 128
H = 128
NCHAIN = 8
N = 1024
CHAIN_MOST = 256
CROP_LO = 64
CROP_HI = 257


def touch_ends(drawn, rng, smallest, top_value):
    spot = [jax.random.randint(jax.random.fold_in(rng, axis), (), 0, length) for axis, length in enumerate(drawn.shape)]
    main_axis = drawn.shape.index(max(drawn.shape))
    neighbour = spot[:main_axis] + [(spot[main_axis] + 1) % drawn.shape[main_axis]] + spot[main_axis + 1:]
    return drawn.at[tuple(spot)].set(smallest).at[tuple(neighbour)].set(top_value)


def block_scale(stream_key, dims, shards, smallest, top_value):
    loudness, own = 1.0, jax.random.fold_in(stream_key, 6)
    for position, parts in shards:
        heights = jnp.exp(jax.random.uniform(jax.random.fold_in(own, position), (parts,), jnp.float32, smallest / len(shards), top_value / len(shards)))
        loudness = loudness * jnp.repeat(heights, dims[position] // parts).reshape([-1 if axis == position else 1 for axis in range(len(dims))])
    return loudness


def length_profile(number_of, total, most, slope):
    portions = [(1 << 20) // math.isqrt(rank ** slope) + 1 for rank in range(2, number_of + 1)]
    spare, given = total - most - (number_of - 1), [1] * (number_of - 1)
    while spare > 0:
        free = [i for i in range(number_of - 1) if given[i] < most]
        whole, left = sum([portions[i] for i in free]), spare
        for i in free:
            addition = min(most - given[i], max(1, left * portions[i] // whole), spare)
            given[i] = given[i] + addition
            spare = spare - addition
    return np.array([most] + given)


def uneven(own_key, number_of, total, reach, slope):
    if number_of == 2:
        one = jax.random.randint(own_key, (), max(1, total - reach), min(reach, total - 1) + 1)
        return jnp.stack([one, total - one])
    lengths = jnp.asarray(length_profile(number_of, total, reach, slope), jnp.int32)
    twos = (number_of - 1) // 2
    donor, receiver = lengths[1:1 + 2 * twos:2], lengths[2:2 + 2 * twos:2]
    room = jnp.minimum(donor - 1, reach - receiver)
    passed = jax.random.randint(jax.random.fold_in(own_key, 1), (twos,), 0, 1 << 20) % (room + 1)
    lengths = lengths.at[1:1 + 2 * twos:2].set(donor - passed).at[2:2 + 2 * twos:2].set(receiver + passed)
    return lengths[jax.random.permutation(jax.random.fold_in(own_key, 2), number_of)]


def bell_draw(rng, shape, scale, most, split=(), kind=jnp.bfloat16):
    values = scale * jax.random.normal(rng, shape, jnp.float32)
    if split:
        values = values * block_scale(rng, shape, split, -0.22, 0.18)
    return jnp.clip(values, -most, most).astype(kind)


def setup_inputs(seed: int = 0) -> dict:
    splits = jax.random.split(jax.random.key(seed), 9)
    pair_rep = bell_draw(splits[0], (N, N, D), 1.0, 6.0, ((0, 128), (1, 4)))
    chain_ids = jnp.searchsorted(jnp.cumsum(uneven(splits[1], NCHAIN, N, CHAIN_MOST, 0)), jnp.arange(N), side="right").astype(jnp.int32)
    crop_lengths = touch_ends(jax.random.randint(splits[2], (NCHAIN,), CROP_LO, CROP_HI), jax.random.fold_in(splits[2], 1), CROP_LO, CROP_HI - 1).astype(jnp.int32)
    ln_in_gain = jnp.clip(1.0 + 0.18 * jax.random.normal(splits[3], (2, D), jnp.float32), 0.1, 1.9)
    w_proj = bell_draw(splits[4], (2, D, 4 * H), D ** -0.5, 0.5)
    w_gate = bell_draw(splits[5], (2, D, D), D ** -0.5, 0.5)
    ln_out_gain = jnp.clip(1.0 + 0.18 * jax.random.normal(splits[6], (2, H), jnp.float32), 0.1, 1.9)
    w_out = bell_draw(splits[7], (2, H, D), H ** -0.5, 0.5)
    return dict(pair_rep=pair_rep, chain_ids=chain_ids, crop_lengths=crop_lengths, ln_in_gain=ln_in_gain, w_proj=w_proj, w_gate=w_gate, ln_out_gain=ln_out_gain, w_out=w_out)


epsilon_norm = 1e-05

def residue_valid(chain_ids, crop_lengths):
    count = chain_ids.shape[0]
    chains = jnp.arange(crop_lengths.shape[0], dtype=jnp.int32)
    member = (chain_ids[:, None] == chains[None, :]).astype(jnp.int32)
    counts = lax.optimization_barrier(jnp.sum(member, axis=0))
    starts = jnp.cumsum(counts) - counts
    first = lax.optimization_barrier(jnp.sum(member * starts[None, :], axis=1))
    limit = lax.optimization_barrier(jnp.sum(member * crop_lengths[None, :], axis=1))
    place = jnp.arange(count, dtype=jnp.int32) - first
    return (place < limit).astype(jnp.float32)

def layer_norm(values, gain, axis):
    centre = lax.optimization_barrier(jnp.mean(values, axis=axis, keepdims=True))
    spread = lax.optimization_barrier(jnp.mean((values - centre) ** 2, axis=axis, keepdims=True))
    return (values - centre) * lax.rsqrt(spread + epsilon_norm) * gain

def update(pair_tile, kept, ln_in, w_proj, w_gate, ln_out, w_out, outgoing):
    count = pair_tile.shape[0]
    width = pair_tile.shape[2]
    hidden = w_out.shape[0]
    block = math.gcd(count, 64)
    blocks = count // block
    pair_blocks = pair_tile.reshape(blocks, block, count, width)
    kept_blocks = kept.reshape(blocks, block)

    def project(items):
        row_block, kept_rows = items
        normed = layer_norm(row_block.astype(jnp.float32), ln_in, 2).astype(jnp.bfloat16)
        projected = jnp.einsum('rqc,cf->frq', normed.astype(jnp.float32), w_proj.astype(jnp.float32))
        pair_mask = kept_rows[:, None] * kept[None, :]
        left_op = (jax.nn.sigmoid(projected[:hidden]) * projected[hidden:2 * hidden] * pair_mask).astype(jnp.bfloat16)
        right_op = (jax.nn.sigmoid(projected[2 * hidden:3 * hidden]) * projected[3 * hidden:] * pair_mask).astype(jnp.bfloat16)
        return (left_op, right_op)
    left_op, right_op = lax.map(project, (pair_blocks, kept_blocks))
    left_op = left_op.transpose(1, 0, 2, 3).reshape(hidden, count, count)
    right_op = right_op.transpose(1, 0, 2, 3).reshape(hidden, count, count)

    def contract(items):
        left_chan = items[0].astype(jnp.float32)
        right_chan = items[1].astype(jnp.float32)
        if outgoing:
            product = jnp.dot(left_chan, right_chan.T)
        else:
            product = jnp.dot(left_chan.T, right_chan)
        return product.astype(jnp.bfloat16)
    triangle = lax.map(contract, (left_op, right_op))
    triangle = lax.optimization_barrier(triangle)
    triangle = triangle.reshape(hidden, blocks, block, count).transpose(1, 0, 2, 3)

    def finish(items):
        row_block, tri_block = items
        normed = layer_norm(row_block.astype(jnp.float32), ln_in, 2).astype(jnp.bfloat16)
        gate_value = jax.nn.sigmoid(jnp.einsum('rqc,cd->rqd', normed.astype(jnp.float32), w_gate.astype(jnp.float32)))
        normed_product = layer_norm(tri_block.astype(jnp.float32), ln_out[:, None, None], 0).astype(jnp.bfloat16)
        update_term = jnp.einsum('hrq,hd->rqd', normed_product.astype(jnp.float32), w_out.astype(jnp.float32))
        return (row_block.astype(jnp.float32) + gate_value * update_term).astype(jnp.bfloat16)
    result = lax.map(finish, (pair_blocks, triangle))
    return result.reshape(count, count, width)

def reference(pair_rep, chain_ids, crop_lengths, ln_in_gain, w_proj, w_gate, ln_out_gain, w_out):
    kept = residue_valid(chain_ids, crop_lengths)
    pair_tile = pair_rep
    for layer_index, outgoing in ((0, True), (1, False)):
        pair_tile = update(pair_tile, kept, ln_in_gain[layer_index], w_proj[layer_index], w_gate[layer_index], ln_out_gain[layer_index], w_out[layer_index], outgoing)
    return pair_tile
```

```python
import functools

import jax
import jax.numpy as jnp
from jax import lax
from jax.experimental import pallas as pl
from jax.experimental.pallas import tpu as pltpu
from jax.sharding import PartitionSpec as P

epsilon_norm = 1e-05
MESH = pl.DeviceIdType.MESH
Z = 16


def residue_valid(chain_ids, crop_lengths):
    count = chain_ids.shape[0]
    chains = jnp.arange(crop_lengths.shape[0], dtype=jnp.int32)
    member = (chain_ids[:, None] == chains[None, :]).astype(jnp.int32)
    counts = jnp.sum(member, axis=0)
    starts = jnp.cumsum(counts) - counts
    first = jnp.sum(member * starts[None, :], axis=1)
    limit = jnp.sum(member * crop_lengths[None, :], axis=1)
    place = jnp.arange(count, dtype=jnp.int32) - first
    return (place < limit).astype(jnp.float32)


def layer_norm(values, gain, axis):
    centre = jnp.mean(values, axis=axis, keepdims=True)
    spread = jnp.mean((values - centre) ** 2, axis=axis, keepdims=True)
    return (values - centre) * lax.rsqrt(spread + epsilon_norm) * gain


def exchange_kernel(n, x_ref, o_ref, send_sem, recv_sem, own_sem):
    me = lax.axis_index("dap")
    planes = n // Z
    z, plane = me % Z, me // Z

    def partner(step):
        return ((plane + step // Z) % planes) * Z + (z + step) % Z

    barrier = pltpu.get_barrier_semaphore()

    def greet(step, carry):
        pl.semaphore_signal(barrier, inc=1, device_id={"dap": partner(step)}, device_id_type=MESH)
        return carry

    lax.fori_loop(1, n, greet, 0)
    own = pltpu.make_async_copy(x_ref.at[me], o_ref.at[me], own_sem)
    own.start()
    pl.semaphore_wait(barrier, n - 1)

    def send(step, carry):
        other = partner(step)
        pltpu.make_async_remote_copy(
            src_ref=x_ref.at[other],
            dst_ref=o_ref.at[me],
            send_sem=send_sem,
            recv_sem=recv_sem,
            device_id={"dap": other},
            device_id_type=MESH,
        ).start()
        return carry

    lax.fori_loop(1, n, send, 0)
    own.wait()
    everything = pltpu.make_async_remote_copy(
        src_ref=x_ref.at[pl.ds(0, n - 1)],
        dst_ref=o_ref.at[pl.ds(0, n - 1)],
        send_sem=send_sem,
        recv_sem=recv_sem,
        device_id={"dap": me},
        device_id_type=MESH,
    )
    everything.wait()


def exchange(x, collective_id):
    n = x.shape[0]
    return pl.pallas_call(
        functools.partial(exchange_kernel, n),
        out_shape=jax.ShapeDtypeStruct(x.shape, x.dtype),
        in_specs=[pl.BlockSpec(memory_space=pltpu.VMEM)],
        out_specs=pl.BlockSpec(memory_space=pltpu.VMEM),
        scratch_shapes=[pltpu.SemaphoreType.DMA, pltpu.SemaphoreType.DMA, pltpu.SemaphoreType.DMA],
        compiler_params=pltpu.CompilerParams(
            collective_id=collective_id, has_side_effects=True, vmem_limit_bytes=16 << 20
        ),
        name="exchange%d" % collective_id,
    )(x)


def column_rows(right_chan):
    return lax.all_to_all(right_chan, "grp", split_axis=0, concat_axis=1, tiled=True)


def update(pair_tile, pair_mask, ln_in, w_proj, w_gate, ln_out, w_out, outgoing):
    hidden = w_out.shape[0]
    rows, columns, _ = pair_tile.shape
    normed = layer_norm(pair_tile.astype(jnp.float32), ln_in, 2).astype(jnp.bfloat16)
    projected = jnp.einsum("rqc,cf->frq", normed, w_proj, preferred_element_type=jnp.float32)
    gate_value = jax.nn.sigmoid(
        jnp.einsum("rqc,cd->rqd", normed, w_gate, preferred_element_type=jnp.float32)
    )
    left_op = (
        jax.nn.sigmoid(projected[:hidden]) * projected[hidden : 2 * hidden] * pair_mask
    ).astype(jnp.bfloat16)
    right_op = (
        jax.nn.sigmoid(projected[2 * hidden : 3 * hidden]) * projected[3 * hidden :] * pair_mask
    ).astype(jnp.bfloat16)
    both = jnp.concatenate(
        [left_op[:, :, :128], left_op[:, :, 128:], right_op[:, :, :128], right_op[:, :, 128:]], axis=1
    )
    got = exchange(both, 0)
    left_chan = jnp.concatenate([got[:, :rows], got[:, rows : 2 * rows]], axis=2).reshape(-1, columns)
    right_chan = jnp.concatenate(
        [got[:, 2 * rows : 3 * rows], got[:, 3 * rows :]], axis=2
    ).reshape(-1, columns)
    left_all = lax.all_gather(left_chan, "grp", axis=1, tiled=True)
    if outgoing:
        triangle = jnp.einsum(
            "ik,jk->ij", left_all, column_rows(right_chan), preferred_element_type=jnp.float32
        )
    else:
        triangle = jnp.einsum("ki,kj->ij", left_all, right_chan, preferred_element_type=jnp.float32)
    triangle = triangle.astype(jnp.bfloat16).reshape(-1, rows, columns)
    back = exchange(jnp.concatenate([triangle[:, :, :128], triangle[:, :, 128:]], axis=1), 1)
    returned = jnp.concatenate([back[:, :rows], back[:, rows:]], axis=2)
    normed_product = layer_norm(returned.astype(jnp.float32), ln_out[:, None, None], 0).astype(
        jnp.bfloat16
    )
    update_term = jnp.einsum(
        "hrq,hd->rqd", normed_product, w_out, preferred_element_type=jnp.float32
    )
    return (pair_tile.astype(jnp.float32) + gate_value * update_term).astype(jnp.bfloat16)


def shards(pair_rep, chain_ids, crop_lengths, ln_in_gain, w_proj, w_gate, ln_out_gain, w_out):
    row_count = pair_rep.shape[0]
    column_count = pair_rep.shape[1]
    kept = residue_valid(chain_ids, crop_lengths)
    row_start = lax.axis_index("dap") * row_count
    column_start = lax.axis_index("grp") * column_count
    kept_rows = lax.dynamic_slice_in_dim(kept, row_start, row_count, 0)
    kept_columns = lax.dynamic_slice_in_dim(kept, column_start, column_count, 0)
    pair_mask = kept_rows[:, None] * kept_columns[None, :]
    pair_tile = pair_rep
    for layer_index, outgoing in ((0, True), (1, False)):
        pair_tile = update(
            pair_tile,
            pair_mask,
            ln_in_gain[layer_index],
            w_proj[layer_index],
            w_gate[layer_index],
            ln_out_gain[layer_index],
            w_out[layer_index],
            outgoing,
        )
    return pair_tile


def solution(mesh):
    placed = (P("dap", "grp", None), P(), P(), P(), P(), P(), P(), P())
    return jax.shard_map(
        shards, mesh=mesh, in_specs=placed, out_specs=P("dap", "grp", None), check_vma=False
    )
```

```python
import functools

import jax
import jax.numpy as jnp
from jax import lax
from jax.experimental import pallas as pl
from jax.experimental.pallas import tpu as pltpu
from jax.sharding import PartitionSpec as P

epsilon_norm = 1e-05
MESH = pl.DeviceIdType.MESH
F32, BF16 = jnp.float32, jnp.bfloat16
Z = 16
PLANES = 8
DAP = Z * PLANES
GRP = 4
GROUPS = 4
SLOTS = DAP // GROUPS
ROWS, COLS, CHAN = 8, 256, 128
BLOCK = SLOTS * ROWS


def residue_valid(chain_ids, crop_lengths):
    count = chain_ids.shape[0]
    chains = jnp.arange(crop_lengths.shape[0], dtype=jnp.int32)
    member = (chain_ids[:, None] == chains[None, :]).astype(jnp.int32)
    counts = jnp.sum(member, axis=0)
    starts = jnp.cumsum(counts) - counts
    first = jnp.sum(member * starts[None, :], axis=1)
    limit = jnp.sum(member * crop_lengths[None, :], axis=1)
    place = jnp.arange(count, dtype=jnp.int32) - first
    return (place < limit).astype(jnp.float32)


def sigmoid(v):
    return 0.5 * jnp.tanh(0.5 * v) + 0.5


def kernel(
    pair_ref, mask_ref, gain_in_ref, w_proj_ref, w_gate_ref, gain_out_ref, w_out_ref,
    out_ref,
    pair_t, normed, gate, staged, right_src, left_src, right_got, left_got,
    right_own, right_mates, left_all, total, tri_src, tri_got, product,
    own_sem, send_sem, right_sem, left_sem, right_mate_sem, left_mate_sem, tri_sem,
):
    me, grp = lax.axis_index("dap"), lax.axis_index("grp")
    z, plane = me % Z, me // Z

    def spot(slot):
        p = slot // PLANES
        half = p // 2
        return 8 + half - (p % 2) * (2 * half + 1), PLANES - 1 - slot % PLANES

    def target(slot):
        along, across = spot(slot)
        return ((plane + across) % PLANES) * Z + (z + along) % Z

    def origin(slot):
        along, across = spot(slot)
        return ((plane + PLANES - across) % PLANES) * Z + (z + Z - along) % Z

    def remote(src, dst, send, recv, dap=None, mate=None):
        device = {"dap": dap} if mate is None else {"grp": mate}
        return pltpu.make_async_remote_copy(
            src_ref=src,
            dst_ref=dst,
            send_sem=send_sem.at[send],
            recv_sem=recv,
            device_id=device,
            device_id_type=MESH,
        )

    def each(lo, hi, body):
        def step(i, carry):
            body(i)
            return carry

        lax.fori_loop(lo, hi, step, 0)

    barrier = pltpu.get_barrier_semaphore()

    def greet(slot):
        pl.semaphore_signal(barrier, inc=1, device_id={"dap": target(slot)}, device_id_type=MESH)

    each(0, DAP - 1, greet)
    for turn in range(1, GRP):
        pl.semaphore_signal(barrier, inc=1, device_id={"grp": (grp + turn) % GRP}, device_id_type=MESH)

    def turn_in(r):
        pair_t[r] = pair_ref[r].astype(F32).T.astype(BF16)

    each(0, ROWS, turn_in)

    def normalise(u):
        def row(r):
            x = pair_t[r].astype(F32)
            centred = x - jnp.mean(x, axis=0, keepdims=True)
            spread = jnp.mean(centred * centred, axis=0, keepdims=True)
            normed[r] = (centred * lax.rsqrt(spread + epsilon_norm) * gain_in_ref[u]).astype(BF16)

        each(0, ROWS, row)

    def operand(u, which, src):
        def row(r):
            both = jnp.dot(w_proj_ref[u, which], normed[r], preferred_element_type=F32)
            value = sigmoid(both[:CHAN]) * both[CHAN:] * mask_ref[pl.ds(r, 1), :]
            staged[pl.ds(r, CHAN, stride=2 * ROWS), :] = value[:, :128]
            staged[pl.ds(ROWS + r, CHAN, stride=2 * ROWS), :] = value[:, 128:]

        each(0, ROWS, row)

        def pack(i):
            rows = staged[pl.ds(pl.multiple_of(i * 256, 256), 256), :]
            src[pl.ds(i * 16, 16)] = rows.reshape(16, 16, 128).astype(BF16)

        each(0, 8, pack)

    def gates(u):
        def row(r):
            gate[r] = sigmoid(jnp.dot(w_gate_ref[u], normed[r], preferred_element_type=F32))

        each(0, ROWS, row)

    def unpack(got, first, dst, row0):
        def some(i):
            tiles = got[pl.ds(first + i * 8, 8)].astype(F32)
            at = pl.ds(pl.multiple_of(row0 + i * 64, 64), 64)
            dst[at, 0:128] = tiles[:, :ROWS].reshape(64, 128).astype(BF16)
            dst[at, 128:256] = tiles[:, ROWS:].reshape(64, 128).astype(BF16)

        each(0, SLOTS // 8, some)

    def send_relative(src, got, send, sems, own):
        for k in range(GROUPS):
            def one(slot):
                other = target(slot)
                remote(src.at[other], got.at[slot], send, sems.at[k], dap=other).start()

            each(k * SLOTS, min((k + 1) * SLOTS, DAP - 1), one)
        pltpu.make_async_copy(src.at[me], got.at[DAP - 1], own).start()

    def wait_group(src, got, sems, own, k):
        count = SLOTS - (k == GROUPS - 1)
        remote(src.at[pl.ds(0, count)], got.at[pl.ds(0, count)], 0, sems.at[k], dap=me).wait_recv()
        if k == GROUPS - 1:
            pltpu.make_async_copy(src.at[me], got.at[DAP - 1], own).wait()

    def sent(src, send):
        everything = src.at[pl.ds(0, DAP - 1)]
        remote(everything, everything, send, tri_sem.at[0], dap=me).wait_send()

    def all_sent(u):
        sent(right_src, 0)
        sent(left_src, 1)
        sent(tri_src, 2)
        shared = left_all.at[u, :, pl.ds(0, GRP - 1)]
        remote(shared, shared, 4, tri_sem.at[0], mate=grp).wait_send()

    def pack_triangle(values, first):
        halves = [values[:, :128].reshape(SLOTS, ROWS, 128), values[:, 128:].reshape(SLOTS, ROWS, 128)]
        tri_src[pl.ds(first, SLOTS)] = jnp.concatenate(halves, axis=1).astype(BF16)

    def finish(u, last):
        remote(
            tri_src.at[pl.ds(0, DAP - 1)], tri_got.at[u, pl.ds(0, DAP - 1)], 2, tri_sem.at[u], dap=me
        ).wait_recv()
        for s in range(2):
            x = tri_got[u, :, s * ROWS : (s + 1) * ROWS].astype(F32)
            centred = x - jnp.mean(x, axis=0, keepdims=True)
            spread = jnp.mean(centred * centred, axis=0, keepdims=True)
            product[s] = (centred * lax.rsqrt(spread + epsilon_norm)).reshape(CHAN * ROWS, 128)

        def row(r):
            across = [product[s, pl.ds(r, CHAN, stride=ROWS), :] for s in range(2)]
            scaled = (jnp.concatenate(across, axis=1) * gain_out_ref[u]).astype(BF16)
            term = jnp.dot(w_out_ref[u], scaled, preferred_element_type=F32)
            result = pair_t[r].astype(F32) + gate[r] * term
            if last:
                out_ref[r] = result.T.astype(BF16)
            else:
                pair_t[r] = result.astype(BF16)

        each(0, ROWS, row)

    normalise(0)
    operand(0, 1, right_src)
    pl.semaphore_wait(barrier, DAP - 1 + GRP - 1)

    def send_right(slot):
        other = target(slot)
        remote(right_src.at[other], right_got.at[0, me], 0, right_sem.at[GROUPS], dap=other).start()

    each(0, DAP - 1, send_right)
    pltpu.make_async_copy(right_src.at[me], right_got.at[0, me], own_sem.at[0]).start()
    operand(0, 0, left_src)
    send_relative(left_src, left_got.at[0], 1, left_sem.at[0], own_sem.at[1])
    gates(0)
    pltpu.make_async_copy(right_src.at[me], right_got.at[0, me], own_sem.at[0]).wait()
    remote(
        right_src.at[pl.ds(0, DAP - 1)], right_got.at[0, pl.ds(0, DAP - 1)], 0, right_sem.at[GROUPS], dap=me
    ).wait_recv()
    for k in range(GRP):
        unpack(right_got.at[0], k * SLOTS, right_own.at[k], 0)
    for turn in range(1, GRP):
        mate = (grp + turn) % GRP
        remote(right_own.at[mate], right_mates.at[grp], 3, right_mate_sem, mate=mate).start()
    right_mates[grp] = right_own[grp]

    def share_left(u, k):
        for turn in range(1, GRP):
            mate = (grp + turn) % GRP
            remote(left_all.at[u, k, grp], left_all.at[u, k, grp], 4, left_mate_sem.at[u, k], mate=mate).start()

    def wait_mates(u, k):
        three = left_all.at[u, k, pl.ds(0, GRP - 1)]
        remote(three, three, 4, left_mate_sem.at[u, k], mate=grp).wait_recv()

    def take_left(k):
        wait_group(left_src, left_got.at[0], left_sem.at[0], own_sem.at[1], k)
        unpack(left_got.at[0], k * SLOTS, left_all.at[0, k, grp], 0)
        share_left(0, k)

    def return_rows(k):
        wait_mates(0, k)
        value = jnp.zeros((BLOCK, COLS), F32)
        for q in range(GRP):
            value += lax.dot_general(
                left_all[0, k, q], right_mates[q], (((1,), (1,)), ((), ())), preferred_element_type=F32
            )
        pack_triangle(value, k * SLOTS)

        def one(slot):
            remote(tri_src.at[slot], tri_got.at[0, me], 2, tri_sem.at[0], dap=origin(slot)).start()

        each(k * SLOTS, min((k + 1) * SLOTS, DAP - 1), one)

    take_left(0)
    three = right_mates.at[pl.ds(0, GRP - 1)]
    remote(three, three, 3, right_mate_sem, mate=grp).wait_recv()
    for k in range(1, GROUPS):
        take_left(k)
        return_rows(k - 1)
    return_rows(GROUPS - 1)
    own_triangle = pltpu.make_async_copy(tri_src.at[DAP - 1], tri_got.at[0, me], own_sem.at[2])
    own_triangle.start()
    own_triangle.wait()
    finish(0, False)
    all_sent(0)
    remote(three, three, 3, right_mate_sem, mate=grp).wait_send()

    normalise(1)
    operand(1, 0, left_src)
    send_relative(left_src, left_got.at[1], 1, left_sem.at[1], own_sem.at[3])
    operand(1, 1, right_src)
    send_relative(right_src, right_got.at[1], 0, right_sem, own_sem.at[4])
    gates(1)
    for k in range(GROUPS):
        wait_group(left_src, left_got.at[1], left_sem.at[1], own_sem.at[3], k)
        unpack(left_got.at[1], k * SLOTS, right_own.at[0], 0)
        left_all[1, k, grp] = right_own[0].astype(F32).T.astype(BF16)
        share_left(1, k)
    for k in range(GROUPS):
        wait_group(right_src, right_got.at[1], right_sem, own_sem.at[4], k)
        unpack(right_got.at[1], k * SLOTS, right_own.at[1], 0)
        wait_mates(1, k)
        for q in range(GRP):
            part = jnp.dot(left_all[1, k, q], right_own[1], preferred_element_type=F32)
            if k == 0:
                total[q] = part
            elif k < GROUPS - 1:
                total[q] += part
            else:
                pack_triangle(total[q] + part, q * SLOTS)

    def send_back(slot):
        other = target(slot)
        remote(tri_src.at[other], tri_got.at[1, me], 2, tri_sem.at[1], dap=other).start()

    each(0, DAP - 1, send_back)
    own_triangle = pltpu.make_async_copy(tri_src.at[me], tri_got.at[1, me], own_sem.at[5])
    own_triangle.start()
    own_triangle.wait()
    finish(1, True)
    all_sent(1)


def shards(pair_rep, chain_ids, crop_lengths, ln_in_gain, w_proj, w_gate, ln_out_gain, w_out):
    kept = residue_valid(chain_ids, crop_lengths)
    kept_rows = lax.dynamic_slice_in_dim(kept, lax.axis_index("dap") * ROWS, ROWS, 0)
    kept_columns = lax.dynamic_slice_in_dim(kept, lax.axis_index("grp") * COLS, COLS, 0)
    pair_mask = kept_rows[:, None] * kept_columns[None, :]
    w_proj_t = w_proj.transpose(0, 2, 1).reshape(2, 2, 2 * CHAN, CHAN)
    vmem = pl.BlockSpec(memory_space=pltpu.VMEM)
    tiles = (DAP, 2 * ROWS, 128)
    return pl.pallas_call(
        kernel,
        out_shape=jax.ShapeDtypeStruct(pair_rep.shape, BF16),
        in_specs=[vmem] * 7,
        out_specs=vmem,
        scratch_shapes=[
            pltpu.VMEM((ROWS, CHAN, COLS), BF16),
            pltpu.VMEM((ROWS, CHAN, COLS), BF16),
            pltpu.VMEM((ROWS, CHAN, COLS), F32),
            pltpu.VMEM((CHAN * 2 * ROWS, 128), F32),
            pltpu.VMEM(tiles, BF16),
            pltpu.VMEM(tiles, BF16),
            pltpu.VMEM((2,) + tiles, BF16),
            pltpu.VMEM((2,) + tiles, BF16),
            pltpu.VMEM((GRP, BLOCK, COLS), BF16),
            pltpu.VMEM((GRP, BLOCK, COLS), BF16),
            pltpu.VMEM((2, GROUPS, GRP, BLOCK, COLS), BF16),
            pltpu.VMEM((GRP, BLOCK, COLS), F32),
            pltpu.VMEM(tiles, BF16),
            pltpu.VMEM((2,) + tiles, BF16),
            pltpu.VMEM((2, CHAN * ROWS, 128), F32),
            pltpu.SemaphoreType.DMA((6,)),
            pltpu.SemaphoreType.DMA((5,)),
            pltpu.SemaphoreType.DMA((GROUPS + 1,)),
            pltpu.SemaphoreType.DMA((2, GROUPS)),
            pltpu.SemaphoreType.DMA,
            pltpu.SemaphoreType.DMA((2, GROUPS)),
            pltpu.SemaphoreType.DMA((2,)),
        ],
        compiler_params=pltpu.CompilerParams(
            collective_id=0, has_side_effects=True, vmem_limit_bytes=40 << 20
        ),
        name="triangles",
    )(
        pair_rep,
        pair_mask,
        ln_in_gain[:, :, None],
        w_proj_t,
        w_gate.transpose(0, 2, 1),
        ln_out_gain[:, :, None],
        w_out.transpose(0, 2, 1),
    )


def solution(mesh):
    placed = (P("dap", "grp", None), P(), P(), P(), P(), P(), P(), P())
    return jax.shard_map(
        shards, mesh=mesh, in_specs=placed, out_specs=P("dap", "grp", None), check_vma=False
    )
```

```python
import functools

import jax
import jax.numpy as jnp
from jax import lax
from jax.experimental import pallas as pl
from jax.experimental.pallas import tpu as pltpu
from jax.sharding import PartitionSpec as P

epsilon_norm = 1e-05
MESH = pl.DeviceIdType.MESH
F32, BF16 = jnp.float32, jnp.bfloat16
Z = 16
PLANES = 8
DAP = Z * PLANES
GRP = 4
GROUPS = 4
SLOTS = DAP // GROUPS
ROWS, COLS, CHAN = 8, 256, 128
BLOCK = SLOTS * ROWS
HALF = COLS // 2


def residue_valid(chain_ids, crop_lengths):
    count = chain_ids.shape[0]
    chains = jnp.arange(crop_lengths.shape[0], dtype=jnp.int32)
    member = (chain_ids[:, None] == chains[None, :]).astype(jnp.int32)
    counts = jnp.sum(member, axis=0)
    starts = jnp.cumsum(counts) - counts
    first = jnp.sum(member * starts[None, :], axis=1)
    limit = jnp.sum(member * crop_lengths[None, :], axis=1)
    place = jnp.arange(count, dtype=jnp.int32) - first
    return (place < limit).astype(jnp.float32)


def sigmoid(v):
    return 0.5 * jnp.tanh(0.5 * v) + 0.5


def kernel(
    pair_ref, mask_ref, gain_in_ref, w_proj_ref, w_gate_ref, gain_out_ref, w_out_ref,
    out_ref,
    pair_t, normed, gate, staged, product,
    right_src, left_src, right_got, left_got, right_own, right_mates, left_all, tri_src, tri_got,
    both_src, both_got, late_src, late_got, unpacked, left_t, right_m,
    own_sem, send_sem, right_sem, left_sem, right_mate_sem, left_mate_sem, tri_sem,
    both_sem, late_left_sem, late_right_sem, turned_sem,
):
    me, grp = lax.axis_index("dap"), lax.axis_index("grp")
    z, plane = me % Z, me // Z

    def spot(slot):
        p = slot // PLANES
        half = p // 2
        return 8 + half - (p % 2) * (2 * half + 1), PLANES - 1 - slot % PLANES

    def target(slot):
        along, across = spot(slot)
        return ((plane + across) % PLANES) * Z + (z + along) % Z

    def origin(slot):
        along, across = spot(slot)
        return ((plane + PLANES - across) % PLANES) * Z + (z + Z - along) % Z

    def remote(src, dst, send, recv, dap=None, mate=None):
        device = {"dap": dap} if mate is None else {"grp": mate}
        return pltpu.make_async_remote_copy(
            src_ref=src,
            dst_ref=dst,
            send_sem=send_sem.at[send],
            recv_sem=recv,
            device_id=device,
            device_id_type=MESH,
        )

    def each(lo, hi, body):
        def step(i, carry):
            body(i)
            return carry

        lax.fori_loop(lo, hi, step, 0)

    def received(ref, sem):
        remote(ref, ref, 0, sem, dap=me).wait_recv()

    def sent(ref, send):
        remote(ref, ref, send, right_sem, dap=me).wait_send()

    def own_copy(src, dst, sem):
        return pltpu.make_async_copy(src, dst, own_sem.at[sem])

    barrier = pltpu.get_barrier_semaphore()

    def greet(slot):
        pl.semaphore_signal(barrier, inc=1, device_id={"dap": target(slot)}, device_id_type=MESH)

    each(0, DAP - 1, greet)
    for turn in range(1, GRP):
        pl.semaphore_signal(barrier, inc=1, device_id={"grp": (grp + turn) % GRP}, device_id_type=MESH)

    def turn_in(r):
        for s in range(2):
            pair_t[s, r] = pair_ref[r, s * HALF : (s + 1) * HALF].astype(F32).T.astype(BF16)

    each(0, ROWS, turn_in)

    def normalise(u, s):
        def row(r):
            x = pair_t[s, r].astype(F32)
            centred = x - jnp.mean(x, axis=0, keepdims=True)
            spread = jnp.mean(centred * centred, axis=0, keepdims=True)
            normed[s, r] = (centred * lax.rsqrt(spread + epsilon_norm) * gain_in_ref[u]).astype(BF16)

        each(0, ROWS, row)

    def operand(u, which, s, first, stride):
        def row(r):
            both = jnp.dot(w_proj_ref[u, which], normed[s, r], preferred_element_type=F32)
            value = sigmoid(both[:CHAN]) * both[CHAN:] * mask_ref[s, r]
            staged[pl.ds(first + r, CHAN, stride=stride), :] = value

        each(0, ROWS, row)

    def pack(src, stride):
        def some(i):
            rows = staged[pl.ds(pl.multiple_of(i * 16 * stride, 128), 16 * stride), :]
            src[pl.ds(i * 16, 16)] = rows.reshape(16, stride, 128).astype(BF16)

        each(0, CHAN // 16, some)

    def gates(u, s):
        def row(r):
            gate[s, r] = sigmoid(jnp.dot(w_gate_ref[u], normed[s, r], preferred_element_type=F32))

        each(0, ROWS, row)

    def send_slots(src, got, send, sem_of, lo, hi):
        def one(slot):
            other = target(slot)
            remote(src.at[other], got.at[slot], send, sem_of, dap=other).start()

        each(lo, hi, one)

    def send_groups(src, got, send, sems, own):
        for k in range(GROUPS):
            send_slots(src, got, send, sems.at[k], k * SLOTS, min((k + 1) * SLOTS, DAP - 1))
        own_copy(src.at[me], got.at[DAP - 1], own).start()

    def wait_group(src, got, sems, own, k):
        received(got.at[pl.ds(0, SLOTS - (k == GROUPS - 1))], sems.at[k])
        if k == GROUPS - 1:
            own_copy(src.at[me], got.at[DAP - 1], own).wait()

    def finish(u, s, last):
        received(tri_got.at[u, s, pl.ds(0, DAP - 1)], tri_sem.at[u, s])
        x = tri_got[u, s].astype(F32)
        centred = x - jnp.mean(x, axis=0, keepdims=True)
        spread = jnp.mean(centred * centred, axis=0, keepdims=True)
        product[...] = (centred * lax.rsqrt(spread + epsilon_norm)).reshape(CHAN * ROWS, 128)

        def row(r):
            scaled = (product[pl.ds(r, CHAN, stride=ROWS), :] * gain_out_ref[u]).astype(BF16)
            term = jnp.dot(w_out_ref[u], scaled, preferred_element_type=F32)
            result = pair_t[s, r].astype(F32) + gate[s, r] * term
            if last:
                out_ref[r, s * HALF : (s + 1) * HALF] = result.T.astype(BF16)
            else:
                pair_t[s, r] = result.astype(BF16)

        each(0, ROWS, row)

    for s in range(2):
        normalise(0, s)
        operand(0, 1, s, s * ROWS, 2 * ROWS)
    pack(right_src, 2 * ROWS)
    pl.semaphore_wait(barrier, DAP - 1 + GRP - 1)

    def send_right(slot):
        other = target(slot)
        remote(right_src.at[other], right_got.at[me], 0, right_sem, dap=other).start()

    each(0, DAP - 1, send_right)
    own_copy(right_src.at[me], right_got.at[me], 0).start()
    for s in range(2):
        operand(0, 0, s, s * ROWS, 2 * ROWS)
    pack(left_src, 2 * ROWS)
    send_groups(left_src, left_got, 1, left_sem, 1)
    for s in range(2):
        gates(0, s)

    def unpack_wide(got, first, dst):
        def some(i):
            tiles = got[pl.ds(first + i * 8, 8)].astype(F32)
            at = pl.ds(pl.multiple_of(i * 64, 64), 64)
            dst[at, 0:HALF] = tiles[:, :ROWS].reshape(64, HALF).astype(BF16)
            dst[at, HALF:COLS] = tiles[:, ROWS:].reshape(64, HALF).astype(BF16)

        each(0, SLOTS // 8, some)

    own_copy(right_src.at[me], right_got.at[me], 0).wait()
    received(right_got.at[pl.ds(0, DAP - 1)], right_sem)
    for q in range(GRP):
        unpack_wide(right_got, q * SLOTS, right_own.at[q])
    for turn in range(1, GRP):
        mate = (grp + turn) % GRP
        remote(right_own.at[mate], right_mates.at[grp], 3, right_mate_sem, mate=mate).start()
    right_mates[grp] = right_own[grp]

    def take_left(k):
        wait_group(left_src, left_got, left_sem, 1, k)
        unpack_wide(left_got, k * SLOTS, left_all.at[k, grp])
        for turn in range(1, GRP):
            mate = (grp + turn) % GRP
            remote(left_all.at[k, grp], left_all.at[k, grp], 4, left_mate_sem.at[k], mate=mate).start()

    def rows_of(k):
        received(left_all.at[k, pl.ds(0, GRP - 1)], left_mate_sem.at[k])
        value = jnp.zeros((BLOCK, COLS), F32)
        for q in range(GRP):
            value += lax.dot_general(
                left_all[k, q], right_mates[q], (((1,), (1,)), ((), ())), preferred_element_type=F32
            )
        for s in range(2):
            part = value[:, s * HALF : (s + 1) * HALF].reshape(SLOTS, ROWS, HALF)
            tri_src[0, s, pl.ds(k * SLOTS, SLOTS)] = part.astype(BF16)

    def return_rows(k, s):
        def one(slot):
            remote(tri_src.at[0, s, slot], tri_got.at[0, s, me], 2, tri_sem.at[0, s], dap=origin(slot)).start()

        each(k * SLOTS, min((k + 1) * SLOTS, DAP - 1), one)

    take_left(0)
    received(right_mates.at[pl.ds(0, GRP - 1)], right_mate_sem)
    for k in range(1, GROUPS):
        take_left(k)
        rows_of(k - 1)
        return_rows(k - 1, 0)
    return_rows(0, 1)
    rows_of(GROUPS - 1)
    return_rows(GROUPS - 1, 0)
    for k in range(1, GROUPS):
        return_rows(k, 1)
    for s in range(2):
        own_triangle = own_copy(tri_src.at[0, s, DAP - 1], tri_got.at[0, s, me], 2)
        own_triangle.start()
        own_triangle.wait()

    finish(0, 0, False)
    normalise(1, 0)
    for which in range(2):
        operand(1, which, 0, which * ROWS, 2 * ROWS)
    pack(both_src, 2 * ROWS)
    send_groups(both_src, both_got, 5, both_sem, 3)
    finish(0, 1, False)
    normalise(1, 1)
    operand(1, 0, 1, 0, ROWS)
    pack(late_src.at[0], ROWS)
    send_groups(late_src.at[0], late_got.at[0], 6, late_left_sem, 4)
    operand(1, 1, 1, 0, ROWS)
    pack(late_src.at[1], ROWS)
    send_slots(late_src.at[1], late_got.at[1], 7, late_right_sem, 0, DAP - 1)
    own_copy(late_src.at[1, me], late_got.at[1, DAP - 1], 5).start()
    for s in range(2):
        gates(1, s)

    def unpack(got, first, count, top, dst, row0):
        def some(i):
            tiles = got[pl.ds(first + i * 8, 8)].astype(F32)[:, top : top + ROWS]
            dst[pl.ds(pl.multiple_of(row0 + i * 64, 64), 64), :] = tiles.reshape(64, HALF).astype(BF16)

        each(0, count // 8, some)

    def share_turned(s, k):
        at = pl.ds(k * BLOCK, BLOCK)
        left_t[s, grp, :, at] = unpacked[...].astype(F32).T.astype(BF16)
        for turn in range(1, GRP):
            mate = (grp + turn) % GRP
            part = left_t.at[s, grp, :, at]
            remote(part, part, 8, turned_sem.at[s], mate=mate).start()

    def quadrant(rows_half, s):
        for q in range(GRP):
            value = jnp.dot(left_t[rows_half, q], right_m[s], preferred_element_type=F32)
            first = (2 * q + rows_half) * Z
            tri_src[1, s, pl.ds(first, Z)] = value.reshape(Z, ROWS, HALF).astype(BF16)

    def return_quadrant(rows_half, s):
        odd = (plane + rows_half) % 2

        def one(i):
            along, _ = spot((i // 4) * PLANES)
            across = 2 * (3 - i % 4) + odd
            other = ((plane + across) % PLANES) * Z + (z + along) % Z
            remote(tri_src.at[1, s, other], tri_got.at[1, s, me], 9, tri_sem.at[1, s], dap=other).start()

        each(0, 4 * Z - 1, one)

        @pl.when(odd == 1)
        def _():
            one(4 * Z - 1)

    def keep_own(s):
        own_triangle = own_copy(tri_src.at[1, s, me], tri_got.at[1, s, me], 6)
        own_triangle.start()
        own_triangle.wait()

    for k in range(GROUPS):
        wait_group(both_src, both_got, both_sem, 3, k)
        unpack(both_got, k * SLOTS, SLOTS, 0, unpacked, 0)
        share_turned(0, k)
        unpack(both_got, k * SLOTS, SLOTS, ROWS, right_m.at[0], k * BLOCK)
    received(left_t.at[0, pl.ds(0, GRP - 1)], turned_sem.at[0])
    quadrant(0, 0)
    return_quadrant(0, 0)
    for k in range(GROUPS):
        wait_group(late_src.at[0], late_got.at[0], late_left_sem, 4, k)
        unpack(late_got.at[0], k * SLOTS, SLOTS, 0, unpacked, 0)
        share_turned(1, k)
    received(left_t.at[1, pl.ds(0, GRP - 1)], turned_sem.at[1])
    quadrant(1, 0)
    return_quadrant(1, 0)
    keep_own(0)
    own_copy(late_src.at[1, me], late_got.at[1, DAP - 1], 5).wait()
    received(late_got.at[1, pl.ds(0, DAP - 1)], late_right_sem)
    unpack(late_got.at[1], 0, DAP, 0, right_m.at[1], 0)
    for rows_half in range(2):
        quadrant(rows_half, 1)
        return_quadrant(rows_half, 1)
    keep_own(1)
    finish(1, 0, True)
    finish(1, 1, True)

    most = pl.ds(0, DAP - 1)
    sent(right_src.at[most], 0)
    sent(left_src.at[most], 1)
    sent(right_mates.at[pl.ds(0, GRP - 1)], 3)
    sent(left_all.at[:, pl.ds(0, GRP - 1)], 4)
    sent(both_src.at[most], 5)
    sent(late_src.at[0, most], 6)
    sent(late_src.at[1, most], 7)
    sent(left_t.at[:, pl.ds(0, GRP - 1)], 8)
    sent(tri_src.at[0, :, most], 2)
    sent(tri_src.at[1, :, most], 9)


def shards(pair_rep, chain_ids, crop_lengths, ln_in_gain, w_proj, w_gate, ln_out_gain, w_out):
    kept = residue_valid(chain_ids, crop_lengths)
    kept_rows = lax.dynamic_slice_in_dim(kept, lax.axis_index("dap") * ROWS, ROWS, 0)
    kept_columns = lax.dynamic_slice_in_dim(kept, lax.axis_index("grp") * COLS, COLS, 0)
    pair_mask = kept_rows[None, :, None, None] * kept_columns.reshape(2, 1, 1, HALF)
    w_proj_t = w_proj.transpose(0, 2, 1).reshape(2, 2, 2 * CHAN, CHAN)
    vmem = pl.BlockSpec(memory_space=pltpu.VMEM)
    wide, narrow = (DAP, 2 * ROWS, 128), (DAP, ROWS, 128)
    turned = (2, ROWS, CHAN, HALF)
    square = (BLOCK, COLS)
    dma = pltpu.SemaphoreType.DMA
    return pl.pallas_call(
        kernel,
        out_shape=jax.ShapeDtypeStruct(pair_rep.shape, BF16),
        in_specs=[vmem] * 7,
        out_specs=vmem,
        scratch_shapes=[
            pltpu.VMEM(turned, BF16),
            pltpu.VMEM(turned, BF16),
            pltpu.VMEM(turned, F32),
            pltpu.VMEM((CHAN * 2 * ROWS, 128), F32),
            pltpu.VMEM((CHAN * ROWS, 128), F32),
            pltpu.VMEM(wide, BF16),
            pltpu.VMEM(wide, BF16),
            pltpu.VMEM(wide, BF16),
            pltpu.VMEM(wide, BF16),
            pltpu.VMEM((GRP,) + square, BF16),
            pltpu.VMEM((GRP,) + square, BF16),
            pltpu.VMEM((GROUPS, GRP) + square, BF16),
            pltpu.VMEM((2, 2) + narrow, BF16),
            pltpu.VMEM((2, 2) + narrow, BF16),
            pltpu.VMEM(wide, BF16),
            pltpu.VMEM(wide, BF16),
            pltpu.VMEM((2,) + narrow, BF16),
            pltpu.VMEM((2,) + narrow, BF16),
            pltpu.VMEM((BLOCK, HALF), BF16),
            pltpu.VMEM((2, GRP, HALF, DAP * ROWS), BF16),
            pltpu.VMEM((2, DAP * ROWS, HALF), BF16),
            dma((7,)),
            dma((10,)),
            dma,
            dma((GROUPS,)),
            dma,
            dma((GROUPS,)),
            dma((2, 2)),
            dma((GROUPS,)),
            dma((GROUPS,)),
            dma,
            dma((2,)),
        ],
        compiler_params=pltpu.CompilerParams(
            collective_id=0, has_side_effects=True, vmem_limit_bytes=40 << 20
        ),
        name="triangles",
    )(
        pair_rep,
        pair_mask,
        ln_in_gain[:, :, None],
        w_proj_t,
        w_gate.transpose(0, 2, 1),
        ln_out_gain[:, :, None],
        w_out.transpose(0, 2, 1),
    )


def solution(mesh):
    placed = (P("dap", "grp", None), P(), P(), P(), P(), P(), P(), P())
    return jax.shard_map(
        shards, mesh=mesh, in_specs=placed, out_specs=P("dap", "grp", None), check_vma=False
    )
```

```python
import functools

import jax
import jax.numpy as jnp
from jax import lax
from jax.experimental import pallas as pl
from jax.experimental.pallas import tpu as pltpu
from jax.sharding import PartitionSpec as P

epsilon_norm = 1e-05
MESH = pl.DeviceIdType.MESH
F32, BF16 = jnp.float32, jnp.bfloat16
Z = 16
PLANES = 8
DAP = Z * PLANES
GRP = 4
GROUPS = 4
SLOTS = DAP // GROUPS
STEPS = Z // GROUPS
ROWS, COLS, CHAN = 8, 256, 128
BLOCK = SLOTS * ROWS
HALF = COLS // 2


def residue_valid(chain_ids, crop_lengths):
    count = chain_ids.shape[0]
    chains = jnp.arange(crop_lengths.shape[0], dtype=jnp.int32)
    member = (chain_ids[:, None] == chains[None, :]).astype(jnp.int32)
    counts = jnp.sum(member, axis=0)
    starts = jnp.cumsum(counts) - counts
    first = jnp.sum(member * starts[None, :], axis=1)
    limit = jnp.sum(member * crop_lengths[None, :], axis=1)
    place = jnp.arange(count, dtype=jnp.int32) - first
    return (place < limit).astype(jnp.float32)


def sigmoid(v):
    return 0.5 * jnp.tanh(0.5 * v) + 0.5


def kernel(
    pair_ref, mask_ref, gain_in_ref, w_proj_ref, w_gate_ref, gain_out_ref, w_out_ref,
    out_ref,
    pair_t, normed, gate, staged, product,
    right_src, left_src, right_got, left_got, right_own, right_mates, left_all, tri_src, tri_got,
    both_src, both_got, late_src, late_got, unpacked, left_t, right_m,
    own_sem, send_sem, right_sem, left_sem, right_mate_sem, left_mate_sem, tri_sem,
    both_sem, late_left_sem, late_right_sem, turned_sem,
):
    me, grp = lax.axis_index("dap"), lax.axis_index("grp")
    z, plane = lax.rem(me, Z), lax.div(me, Z)

    planes_on = [lax.rem(plane + (PLANES - 1 - a), PLANES) * Z for a in range(PLANES)]
    planes_back = [lax.rem(plane + (a + 1), PLANES) * Z for a in range(PLANES)]

    def along(p):
        half = lax.div(p, 2)
        return 8 + half - lax.rem(p, 2) * (2 * half + 1)

    def slots(lo, hi, body, back=False):
        planes = planes_back if back else planes_on

        def one(p, count):
            there = lax.rem(z + Z - along(p), Z) if back else lax.rem(z + along(p), Z)
            for a in range(count):
                body(p * PLANES + a, planes[a] + there)

        def step(p, carry):
            one(p, PLANES)
            return carry

        lax.fori_loop(lo, min(hi, Z - 1), step, 0)
        if hi == Z:
            one(jnp.int32(Z - 1), PLANES - 1)

    def remote(src, dst, send, recv, dap=None, mate=None):
        device = {"dap": dap} if mate is None else {"grp": mate}
        return pltpu.make_async_remote_copy(
            src_ref=src,
            dst_ref=dst,
            send_sem=send_sem.at[send],
            recv_sem=recv,
            device_id=device,
            device_id_type=MESH,
        )

    def each(lo, hi, body, unroll=4):
        def step(i, carry):
            body(i)
            return carry

        lax.fori_loop(lo, hi, step, 0, unroll=unroll)

    def received(ref, sem):
        remote(ref, ref, 0, sem, dap=me).wait_recv()

    def sent(ref, send):
        remote(ref, ref, send, right_sem, dap=me).wait_send()

    def own_copy(src, dst, sem):
        return pltpu.make_async_copy(src, dst, own_sem.at[sem])

    barrier = pltpu.get_barrier_semaphore()

    def greet(slot, other):
        pl.semaphore_signal(barrier, inc=1, device_id={"dap": other}, device_id_type=MESH)

    slots(0, Z, greet)
    for turn in range(1, GRP):
        pl.semaphore_signal(barrier, inc=1, device_id={"grp": lax.rem(grp + turn, GRP)}, device_id_type=MESH)

    def turn_in(r):
        for s in range(2):
            pair_t[s, r] = pair_ref[r, s * HALF : (s + 1) * HALF].astype(F32).T.astype(BF16)

    each(0, ROWS, turn_in)

    def normalise(u, s):
        def row(r):
            x = pair_t[s, r].astype(F32)
            centred = x - jnp.mean(x, axis=0, keepdims=True)
            spread = jnp.mean(centred * centred, axis=0, keepdims=True)
            normed[s, r] = (centred * lax.rsqrt(spread + epsilon_norm) * gain_in_ref[u]).astype(BF16)

        each(0, ROWS, row)

    def operand(u, which, s, first, stride):
        def row(r):
            both = jnp.dot(w_proj_ref[u, which], normed[s, r], preferred_element_type=F32)
            value = sigmoid(both[:CHAN]) * both[CHAN:] * mask_ref[s, r]
            staged[pl.ds(first + r, CHAN, stride=stride), :] = value

        each(0, ROWS, row)

    def pack(src, stride):
        def some(i):
            rows = staged[pl.ds(pl.multiple_of(i * 16 * stride, 128), 16 * stride), :]
            src[pl.ds(i * 16, 16)] = rows.reshape(16, stride, 128).astype(BF16)

        each(0, CHAN // 16, some)

    def gates(u, s):
        def row(r):
            gate[s, r] = sigmoid(jnp.dot(w_gate_ref[u], normed[s, r], preferred_element_type=F32))

        each(0, ROWS, row)

    def send_slots(src, got, send, sem, lo, hi):
        def one(slot, other):
            remote(src.at[other], got.at[slot], send, sem, dap=other).start()

        slots(lo, hi, one)

    def send_groups(src, got, send, sems, own):
        for k in range(GROUPS):
            send_slots(src, got, send, sems.at[k], k * STEPS, (k + 1) * STEPS)
        own_copy(src.at[me], got.at[DAP - 1], own).start()

    def wait_group(src, got, sems, own, k):
        received(got.at[pl.ds(0, SLOTS - (k == GROUPS - 1))], sems.at[k])
        if k == GROUPS - 1:
            own_copy(src.at[me], got.at[DAP - 1], own).wait()

    def finish(u, s, last):
        received(tri_got.at[u, s, pl.ds(0, DAP - 1)], tri_sem.at[u, s])
        x = tri_got[u, s].astype(F32)
        centred = x - jnp.mean(x, axis=0, keepdims=True)
        spread = jnp.mean(centred * centred, axis=0, keepdims=True)
        product[...] = (centred * lax.rsqrt(spread + epsilon_norm)).reshape(CHAN * ROWS, 128)

        def row(r):
            scaled = (product[pl.ds(r, CHAN, stride=ROWS), :] * gain_out_ref[u]).astype(BF16)
            term = jnp.dot(w_out_ref[u], scaled, preferred_element_type=F32)
            result = pair_t[s, r].astype(F32) + gate[s, r] * term
            if last:
                out_ref[r, s * HALF : (s + 1) * HALF] = result.T.astype(BF16)
            else:
                pair_t[s, r] = result.astype(BF16)

        each(0, ROWS, row)

    for s in range(2):
        normalise(0, s)
        operand(0, 1, s, s * ROWS, 2 * ROWS)
    pack(right_src, 2 * ROWS)
    pl.semaphore_wait(barrier, DAP - 1 + GRP - 1)

    def send_right(slot, other):
        remote(right_src.at[other], right_got.at[me], 0, right_sem, dap=other).start()

    slots(0, Z, send_right)
    own_copy(right_src.at[me], right_got.at[me], 0).start()
    for s in range(2):
        operand(0, 0, s, s * ROWS, 2 * ROWS)
    pack(left_src, 2 * ROWS)
    send_groups(left_src, left_got, 1, left_sem, 1)
    for s in range(2):
        gates(0, s)

    def unpack_wide(got, first, dst):
        def some(i):
            tiles = got[pl.ds(first + i * 8, 8)].astype(F32)
            at = pl.ds(pl.multiple_of(i * 64, 64), 64)
            dst[at, 0:HALF] = tiles[:, :ROWS].reshape(64, HALF).astype(BF16)
            dst[at, HALF:COLS] = tiles[:, ROWS:].reshape(64, HALF).astype(BF16)

        each(0, SLOTS // 8, some)

    own_copy(right_src.at[me], right_got.at[me], 0).wait()
    received(right_got.at[pl.ds(0, DAP - 1)], right_sem)
    for q in range(GRP):
        unpack_wide(right_got, q * SLOTS, right_own.at[q])
    for turn in range(1, GRP):
        mate = lax.rem(grp + turn, GRP)
        remote(right_own.at[mate], right_mates.at[grp], 3, right_mate_sem, mate=mate).start()
    right_mates[grp] = right_own[grp]

    def take_left(k):
        wait_group(left_src, left_got, left_sem, 1, k)
        unpack_wide(left_got, k * SLOTS, left_all.at[k, grp])
        for turn in range(1, GRP):
            mate = lax.rem(grp + turn, GRP)
            remote(left_all.at[k, grp], left_all.at[k, grp], 4, left_mate_sem.at[k], mate=mate).start()

    def rows_of(k):
        received(left_all.at[k, pl.ds(0, GRP - 1)], left_mate_sem.at[k])
        value = jnp.zeros((BLOCK, COLS), F32)
        for q in range(GRP):
            value += lax.dot_general(
                left_all[k, q], right_mates[q], (((1,), (1,)), ((), ())), preferred_element_type=F32
            )
        for s in range(2):
            part = value[:, s * HALF : (s + 1) * HALF].reshape(SLOTS, ROWS, HALF)
            tri_src[0, s, pl.ds(k * SLOTS, SLOTS)] = part.astype(BF16)

    def return_rows(k, s):
        def one(slot, other):
            remote(tri_src.at[0, s, slot], tri_got.at[0, s, me], 2, tri_sem.at[0, s], dap=other).start()

        slots(k * STEPS, (k + 1) * STEPS, one, back=True)

    take_left(0)
    received(right_mates.at[pl.ds(0, GRP - 1)], right_mate_sem)
    for k in range(1, GROUPS):
        take_left(k)
        rows_of(k - 1)
        return_rows(k - 1, 0)
    return_rows(0, 1)
    rows_of(GROUPS - 1)
    return_rows(GROUPS - 1, 0)
    for k in range(1, GROUPS):
        return_rows(k, 1)
    for s in range(2):
        own_triangle = own_copy(tri_src.at[0, s, DAP - 1], tri_got.at[0, s, me], 2)
        own_triangle.start()
        own_triangle.wait()

    finish(0, 0, False)
    normalise(1, 0)
    for which in range(2):
        operand(1, which, 0, which * ROWS, 2 * ROWS)
    pack(both_src, 2 * ROWS)
    send_groups(both_src, both_got, 5, both_sem, 3)
    finish(0, 1, False)
    normalise(1, 1)
    operand(1, 0, 1, 0, ROWS)
    pack(late_src.at[0], ROWS)
    send_groups(late_src.at[0], late_got.at[0], 6, late_left_sem, 4)
    operand(1, 1, 1, 0, ROWS)
    pack(late_src.at[1], ROWS)
    send_slots(late_src.at[1], late_got.at[1], 7, late_right_sem, 0, Z)
    own_copy(late_src.at[1, me], late_got.at[1, DAP - 1], 5).start()
    for s in range(2):
        gates(1, s)

    def unpack(got, first, count, top, dst, row0):
        def some(i):
            tiles = got[pl.ds(first + i * 8, 8)].astype(F32)[:, top : top + ROWS]
            dst[pl.ds(pl.multiple_of(row0 + i * 64, 64), 64), :] = tiles.reshape(64, HALF).astype(BF16)

        each(0, count // 8, some)

    def share_turned(s, k):
        at = pl.ds(k * BLOCK, BLOCK)
        left_t[s, grp, :, at] = unpacked[...].astype(F32).T.astype(BF16)
        for turn in range(1, GRP):
            mate = lax.rem(grp + turn, GRP)
            part = left_t.at[s, grp, :, at]
            remote(part, part, 8, turned_sem.at[s], mate=mate).start()

    def quadrant(rows_half, s):
        for q in range(GRP):
            value = jnp.dot(left_t[rows_half, q], right_m[s], preferred_element_type=F32)
            first = (2 * q + rows_half) * Z
            tri_src[1, s, pl.ds(first, Z)] = value.reshape(Z, ROWS, HALF).astype(BF16)

    def return_quadrant(rows_half, s):
        odd = lax.rem(plane + rows_half, 2)
        planes = [lax.rem(plane + (2 * a + odd), PLANES) * Z for a in (3, 2, 1, 0)]

        def one(other):
            remote(tri_src.at[1, s, other], tri_got.at[1, s, me], 9, tri_sem.at[1, s], dap=other).start()

        def step(p, carry):
            there = lax.rem(z + along(p), Z)
            for first in planes:
                one(first + there)
            return carry

        lax.fori_loop(0, Z - 1, step, 0)
        for first in planes[:3]:
            one(first + z)

        @pl.when(odd == 1)
        def _():
            one(planes[3] + z)

    def keep_own(s):
        own_triangle = own_copy(tri_src.at[1, s, me], tri_got.at[1, s, me], 6)
        own_triangle.start()
        own_triangle.wait()

    for k in range(GROUPS):
        wait_group(both_src, both_got, both_sem, 3, k)
        unpack(both_got, k * SLOTS, SLOTS, 0, unpacked, 0)
        share_turned(0, k)
        unpack(both_got, k * SLOTS, SLOTS, ROWS, right_m.at[0], k * BLOCK)
    received(left_t.at[0, pl.ds(0, GRP - 1)], turned_sem.at[0])
    quadrant(0, 0)
    return_quadrant(0, 0)
    for k in range(GROUPS):
        wait_group(late_src.at[0], late_got.at[0], late_left_sem, 4, k)
        unpack(late_got.at[0], k * SLOTS, SLOTS, 0, unpacked, 0)
        share_turned(1, k)
    received(left_t.at[1, pl.ds(0, GRP - 1)], turned_sem.at[1])
    quadrant(1, 0)
    return_quadrant(1, 0)
    keep_own(0)
    own_copy(late_src.at[1, me], late_got.at[1, DAP - 1], 5).wait()
    received(late_got.at[1, pl.ds(0, DAP - 1)], late_right_sem)
    unpack(late_got.at[1], 0, DAP, 0, right_m.at[1], 0)
    for rows_half in range(2):
        quadrant(rows_half, 1)
        return_quadrant(rows_half, 1)
    keep_own(1)
    finish(1, 0, True)
    finish(1, 1, True)

    most = pl.ds(0, DAP - 1)
    sent(right_src.at[most], 0)
    sent(left_src.at[most], 1)
    sent(right_mates.at[pl.ds(0, GRP - 1)], 3)
    sent(left_all.at[:, pl.ds(0, GRP - 1)], 4)
    sent(both_src.at[most], 5)
    sent(late_src.at[0, most], 6)
    sent(late_src.at[1, most], 7)
    sent(left_t.at[:, pl.ds(0, GRP - 1)], 8)
    sent(tri_src.at[0, :, most], 2)
    sent(tri_src.at[1, :, most], 9)


def shards(pair_rep, chain_ids, crop_lengths, ln_in_gain, w_proj, w_gate, ln_out_gain, w_out):
    kept = residue_valid(chain_ids, crop_lengths)
    kept_rows = lax.dynamic_slice_in_dim(kept, lax.axis_index("dap") * ROWS, ROWS, 0)
    kept_columns = lax.dynamic_slice_in_dim(kept, lax.axis_index("grp") * COLS, COLS, 0)
    pair_mask = kept_rows[None, :, None, None] * kept_columns.reshape(2, 1, 1, HALF)
    w_proj_t = w_proj.transpose(0, 2, 1).reshape(2, 2, 2 * CHAN, CHAN)
    vmem = pl.BlockSpec(memory_space=pltpu.VMEM)
    wide, narrow = (DAP, 2 * ROWS, 128), (DAP, ROWS, 128)
    turned = (2, ROWS, CHAN, HALF)
    square = (BLOCK, COLS)
    dma = pltpu.SemaphoreType.DMA
    return pl.pallas_call(
        kernel,
        out_shape=jax.ShapeDtypeStruct(pair_rep.shape, BF16),
        in_specs=[vmem] * 7,
        out_specs=vmem,
        scratch_shapes=[
            pltpu.VMEM(turned, BF16),
            pltpu.VMEM(turned, BF16),
            pltpu.VMEM(turned, F32),
            pltpu.VMEM((CHAN * 2 * ROWS, 128), F32),
            pltpu.VMEM((CHAN * ROWS, 128), F32),
            pltpu.VMEM(wide, BF16),
            pltpu.VMEM(wide, BF16),
            pltpu.VMEM(wide, BF16),
            pltpu.VMEM(wide, BF16),
            pltpu.VMEM((GRP,) + square, BF16),
            pltpu.VMEM((GRP,) + square, BF16),
            pltpu.VMEM((GROUPS, GRP) + square, BF16),
            pltpu.VMEM((2, 2) + narrow, BF16),
            pltpu.VMEM((2, 2) + narrow, BF16),
            pltpu.VMEM(wide, BF16),
            pltpu.VMEM(wide, BF16),
            pltpu.VMEM((2,) + narrow, BF16),
            pltpu.VMEM((2,) + narrow, BF16),
            pltpu.VMEM((BLOCK, HALF), BF16),
            pltpu.VMEM((2, GRP, HALF, DAP * ROWS), BF16),
            pltpu.VMEM((2, DAP * ROWS, HALF), BF16),
            dma((7,)),
            dma((10,)),
            dma,
            dma((GROUPS,)),
            dma,
            dma((GROUPS,)),
            dma((2, 2)),
            dma((GROUPS,)),
            dma((GROUPS,)),
            dma,
            dma((2,)),
        ],
        compiler_params=pltpu.CompilerParams(
            collective_id=0, has_side_effects=True, vmem_limit_bytes=40 << 20
        ),
        name="triangles",
    )(
        pair_rep,
        pair_mask,
        ln_in_gain[:, :, None],
        w_proj_t,
        w_gate.transpose(0, 2, 1),
        ln_out_gain[:, :, None],
        w_out.transpose(0, 2, 1),
    )


def solution(mesh):
    placed = (P("dap", "grp", None), P(), P(), P(), P(), P(), P(), P())
    return jax.shard_map(
        shards, mesh=mesh, in_specs=placed, out_specs=P("dap", "grp", None), check_vma=False
    )
```

```python
import functools

import jax
import jax.numpy as jnp
from jax import lax
from jax.experimental import pallas as pl
from jax.experimental.pallas import tpu as pltpu
from jax.sharding import PartitionSpec as P

epsilon_norm = 1e-05
MESH = pl.DeviceIdType.MESH
F32, BF16 = jnp.float32, jnp.bfloat16
Z = 16
PLANES = 8
DAP = Z * PLANES
GRP = 4
GROUPS = 4
SLOTS = DAP // GROUPS
STEPS = Z // GROUPS
ROWS, COLS, CHAN = 8, 256, 128
BLOCK = SLOTS * ROWS
HALF = COLS // 2


def sigmoid(v):
    return 0.5 * jnp.tanh(0.5 * v) + 0.5


def kernel(
    pair_hbm, chain_hbm, crop_ref, ln_in_hbm, w_proj_hbm, w_gate_hbm, ln_out_hbm, w_out_hbm,
    out_ref,
    pair_ref, chain_ref, ln_in_ref, w_proj_ref, w_gate_ref, ln_out_ref, w_out_ref,
    kept_ref, mask_ref, gain_in, gain_out, w_proj_t, w_gate_t, w_out_t,
    pair_t, normed, gate, staged, product,
    right_src, left_src, right_got, left_got, right_own, right_mates, left_all, tri_src, tri_got,
    both_src, both_got, late_src, late_got, unpacked, left_t, right_m,
    in_sem, own_sem, send_sem, right_sem, left_sem, right_mate_sem, left_mate_sem, tri_sem,
    both_sem, late_left_sem, late_right_sem, turned_sem,
):
    me, grp = lax.axis_index("dap"), lax.axis_index("grp")
    z, plane = lax.rem(me, Z), lax.div(me, Z)

    planes_on = [lax.rem(plane + (PLANES - 1 - a), PLANES) * Z for a in range(PLANES)]
    planes_back = [lax.rem(plane + (a + 1), PLANES) * Z for a in range(PLANES)]

    def along(p):
        half = lax.div(p, 2)
        return 8 + half - lax.rem(p, 2) * (2 * half + 1)

    def slots(lo, hi, body, back=False):
        planes = planes_back if back else planes_on

        def one(p, count):
            there = lax.rem(z + Z - along(p), Z) if back else lax.rem(z + along(p), Z)
            for a in range(count):
                body(p * PLANES + a, planes[a] + there)

        def step(p, carry):
            one(p, PLANES)
            return carry

        lax.fori_loop(lo, min(hi, Z - 1), step, 0)
        if hi == Z:
            one(jnp.int32(Z - 1), PLANES - 1)

    def remote(src, dst, send, recv, dap=None, mate=None):
        device = {"dap": dap} if mate is None else {"grp": mate}
        return pltpu.make_async_remote_copy(
            src_ref=src,
            dst_ref=dst,
            send_sem=send_sem.at[send],
            recv_sem=recv,
            device_id=device,
            device_id_type=MESH,
        )

    def each(lo, hi, body, unroll=8):
        def step(i, carry):
            body(i)
            return carry

        lax.fori_loop(lo, hi, step, 0, unroll=unroll)

    def received(ref, sem):
        remote(ref, ref, 0, sem, dap=me).wait_recv()

    def sent(ref, send):
        remote(ref, ref, send, right_sem, dap=me).wait_send()

    def own_copy(src, dst, sem):
        return pltpu.make_async_copy(src, dst, own_sem.at[sem])

    inputs = [
        pltpu.make_async_copy(src, dst, in_sem.at[i])
        for i, (src, dst) in enumerate(
            [
                (pair_hbm, pair_ref),
                (chain_hbm, chain_ref),
                (ln_in_hbm, ln_in_ref),
                (w_proj_hbm, w_proj_ref),
                (w_gate_hbm, w_gate_ref),
                (ln_out_hbm, ln_out_ref),
                (w_out_hbm, w_out_ref),
            ]
        )
    ]
    for copy in inputs:
        copy.start()
    barrier = pltpu.get_barrier_semaphore()

    def greet(slot, other):
        pl.semaphore_signal(barrier, inc=1, device_id={"dap": other}, device_id_type=MESH)

    slots(0, Z, greet)
    for turn in range(1, GRP):
        pl.semaphore_signal(barrier, inc=1, device_id={"grp": lax.rem(grp + turn, GRP)}, device_id_type=MESH)

    def turned(block):
        return block.astype(F32).T.astype(BF16)

    def turn_projection(u, which):
        for part in range(2):
            at = (2 * which + part) * CHAN
            w_proj_t[u, which, part * CHAN : (part + 1) * CHAN] = turned(w_proj_ref[u, :, at : at + CHAN])

    def turn_gain(u):
        gain_in[u] = jnp.broadcast_to(ln_in_ref[u : u + 1], (CHAN, CHAN)).T
        gain_out[u] = jnp.broadcast_to(ln_out_ref[u : u + 1], (CHAN, CHAN)).T

    def residue_mask():
        ids = chain_ref[...]
        sublane = lax.broadcasted_iota(jnp.int32, (8, 128), 0)
        lane = lax.broadcasted_iota(jnp.int32, (8, 128), 1)
        place = (sublane * 128 + lane).astype(F32)
        start, first, limit = jnp.zeros((1, 1), F32), jnp.zeros((8, 128), F32), jnp.zeros((8, 128), F32)
        for chain in range(crop_ref.shape[0]):
            member = (ids == chain).astype(F32)
            first += member * start
            limit += member * crop_ref[chain].astype(F32)
            start += jnp.sum(jnp.sum(member, axis=1, keepdims=True), axis=0, keepdims=True)
        kept = (place - first < limit).astype(F32)
        for i in range(8):
            kept_ref[i] = kept[i : i + 1]
        mine = lane == sublane + lax.rem(me, Z) * ROWS
        kept_rows = jnp.sum(jnp.where(mine, kept_ref[plane], 0.0), axis=1, keepdims=True)
        for s in range(2):
            mask = kept_rows * kept_ref[2 * grp + s]
            for r in range(ROWS):
                mask_ref[s, r] = mask[r : r + 1]

    def turn_in(r):
        for s in range(2):
            pair_t[s, r] = turned(pair_ref[r, s * HALF : (s + 1) * HALF])

    for copy in inputs:
        copy.wait()
    each(0, ROWS, turn_in)

    def normalise(u, s):
        def row(r):
            x = pair_t[s, r].astype(F32)
            centred = x - jnp.mean(x, axis=0, keepdims=True)
            spread = jnp.mean(centred * centred, axis=0, keepdims=True)
            normed[s, r] = (centred * lax.rsqrt(spread + epsilon_norm) * gain_in[u]).astype(BF16)

        each(0, ROWS, row)

    def operand(u, which, s, first, stride):
        def row(r):
            both = jnp.dot(w_proj_t[u, which], normed[s, r], preferred_element_type=F32)
            value = sigmoid(both[:CHAN]) * both[CHAN:] * mask_ref[s, r]
            staged[pl.ds(first + r, CHAN, stride=stride), :] = value

        each(0, ROWS, row)

    def operand_wide(which):
        def row(r):
            wide = jnp.concatenate([normed[0, r], normed[1, r]], axis=1)
            both = jnp.dot(w_proj_t[0, which], wide, preferred_element_type=F32)
            value = sigmoid(both[:CHAN]) * both[CHAN:]
            for s in range(2):
                half = value[:, s * HALF : (s + 1) * HALF] * mask_ref[s, r]
                staged[pl.ds(s * ROWS + r, CHAN, stride=2 * ROWS), :] = half

        each(0, ROWS, row)

    def pack(src, stride):
        def some(i):
            rows = staged[pl.ds(pl.multiple_of(i * 16 * stride, 128), 16 * stride), :]
            src[pl.ds(i * 16, 16)] = rows.reshape(16, stride, 128).astype(BF16)

        each(0, CHAN // 16, some)

    def gates(u, s):
        def row(r):
            gate[s, r] = sigmoid(jnp.dot(w_gate_t[u], normed[s, r], preferred_element_type=F32))

        each(0, ROWS, row)

    def send_slots(src, got, send, sem, lo, hi):
        def one(slot, other):
            remote(src.at[other], got.at[slot], send, sem, dap=other).start()

        slots(lo, hi, one)

    def send_groups(src, got, send, sems, own):
        for k in range(GROUPS):
            send_slots(src, got, send, sems.at[k], k * STEPS, (k + 1) * STEPS)
        own_copy(src.at[me], got.at[DAP - 1], own).start()

    def wait_group(src, got, sems, own, k):
        received(got.at[pl.ds(0, SLOTS - (k == GROUPS - 1))], sems.at[k])
        if k == GROUPS - 1:
            own_copy(src.at[me], got.at[DAP - 1], own).wait()

    def finish(u, s, last):
        received(tri_got.at[u, s, pl.ds(0, DAP - 1)], tri_sem.at[u, s])
        x = tri_got[u, s].astype(F32)
        centred = x - jnp.mean(x, axis=0, keepdims=True)
        spread = jnp.mean(centred * centred, axis=0, keepdims=True)
        product[pl.ds(0, CHAN * ROWS), :] = (centred * lax.rsqrt(spread + epsilon_norm)).reshape(CHAN * ROWS, 128)

        def row(r):
            scaled = (product[pl.ds(r, CHAN, stride=ROWS), :] * gain_out[u]).astype(BF16)
            term = jnp.dot(w_out_t[u], scaled, preferred_element_type=F32)
            result = pair_t[s, r].astype(F32) + gate[s, r] * term
            if last:
                out_ref[r, s * HALF : (s + 1) * HALF] = result.T.astype(BF16)
            else:
                pair_t[s, r] = result.astype(BF16)

        each(0, ROWS, row)

    residue_mask()
    turn_gain(0)
    turn_projection(0, 1)
    for s in range(2):
        normalise(0, s)
    operand_wide(1)
    pack(right_src, 2 * ROWS)
    pl.semaphore_wait(barrier, DAP - 1 + GRP - 1)

    def send_right(slot, other):
        remote(right_src.at[other], right_got.at[me], 0, right_sem, dap=other).start()

    slots(0, Z, send_right)
    own_copy(right_src.at[me], right_got.at[me], 0).start()
    turn_projection(0, 0)
    operand_wide(0)
    pack(left_src, 2 * ROWS)
    send_groups(left_src, left_got, 1, left_sem, 1)
    for u in range(2):
        w_gate_t[u] = turned(w_gate_ref[u])
        w_out_t[u] = turned(w_out_ref[u])
    for s in range(2):
        gates(0, s)
    turn_gain(1)
    for which in range(2):
        turn_projection(1, which)

    def unpack_wide(got, first, dst):
        def some(i):
            tiles = got[pl.ds(first + i * 8, 8)].astype(F32)
            at = pl.ds(pl.multiple_of(i * 64, 64), 64)
            dst[at, 0:HALF] = tiles[:, :ROWS].reshape(64, HALF).astype(BF16)
            dst[at, HALF:COLS] = tiles[:, ROWS:].reshape(64, HALF).astype(BF16)

        each(0, SLOTS // 8, some)

    own_copy(right_src.at[me], right_got.at[me], 0).wait()
    received(right_got.at[pl.ds(0, DAP - 1)], right_sem)
    for q in range(GRP):
        unpack_wide(right_got, q * SLOTS, right_own.at[q])
    for turn in range(1, GRP):
        mate = lax.rem(grp + turn, GRP)
        remote(right_own.at[mate], right_mates.at[grp], 3, right_mate_sem, mate=mate).start()
    right_mates[grp] = right_own[grp]

    def take_left(k):
        wait_group(left_src, left_got, left_sem, 1, k)
        unpack_wide(left_got, k * SLOTS, left_all.at[k, grp])
        for turn in range(1, GRP):
            mate = lax.rem(grp + turn, GRP)
            remote(left_all.at[k, grp], left_all.at[k, grp], 4, left_mate_sem.at[k], mate=mate).start()

    def rows_of(k):
        received(left_all.at[k, pl.ds(0, GRP - 1)], left_mate_sem.at[k])
        value = jnp.zeros((BLOCK, COLS), F32)
        for q in range(GRP):
            value += lax.dot_general(
                left_all[k, q], right_mates[q], (((1,), (1,)), ((), ())), preferred_element_type=F32
            )
        for s in range(2):
            part = value[:, s * HALF : (s + 1) * HALF].reshape(SLOTS, ROWS, HALF)
            tri_src[0, s, pl.ds(k * SLOTS, SLOTS)] = part.astype(BF16)

    def return_rows(k, s):
        def one(slot, other):
            remote(tri_src.at[0, s, slot], tri_got.at[0, s, me], 2, tri_sem.at[0, s], dap=other).start()

        slots(k * STEPS, (k + 1) * STEPS, one, back=True)

    take_left(0)
    received(right_mates.at[pl.ds(0, GRP - 1)], right_mate_sem)
    for k in range(1, GROUPS):
        take_left(k)
        rows_of(k - 1)
        return_rows(k - 1, 0)
    return_rows(0, 1)
    rows_of(GROUPS - 1)
    return_rows(GROUPS - 1, 0)
    for k in range(1, GROUPS):
        return_rows(k, 1)
    for s in range(2):
        own_triangle = own_copy(tri_src.at[0, s, DAP - 1], tri_got.at[0, s, me], 2)
        own_triangle.start()
        own_triangle.wait()

    finish(0, 0, False)
    normalise(1, 0)
    for which in range(2):
        operand(1, which, 0, which * ROWS, 2 * ROWS)
    pack(both_src, 2 * ROWS)
    send_groups(both_src, both_got, 5, both_sem, 3)
    finish(0, 1, False)
    normalise(1, 1)
    operand(1, 0, 1, 0, ROWS)
    pack(late_src.at[0], ROWS)
    send_groups(late_src.at[0], late_got.at[0], 6, late_left_sem, 4)
    operand(1, 1, 1, 0, ROWS)
    pack(late_src.at[1], ROWS)
    send_slots(late_src.at[1], late_got.at[1], 7, late_right_sem, 0, Z)
    own_copy(late_src.at[1, me], late_got.at[1, DAP - 1], 5).start()
    for s in range(2):
        gates(1, s)

    def unpack(got, first, count, top, dst, row0):
        def some(i):
            tiles = got[pl.ds(first + i * 8, 8)].astype(F32)[:, top : top + ROWS]
            dst[pl.ds(pl.multiple_of(row0 + i * 64, 64), 64), :] = tiles.reshape(64, HALF).astype(BF16)

        each(0, count // 8, some)

    def share_turned(s, k):
        at = pl.ds(k * BLOCK, BLOCK)
        left_t[s, grp, :, at] = unpacked[...].astype(F32).T.astype(BF16)
        for turn in range(1, GRP):
            mate = lax.rem(grp + turn, GRP)
            part = left_t.at[s, grp, :, at]
            remote(part, part, 8, turned_sem.at[s], mate=mate).start()

    def quadrant(rows_half, s):
        for q in range(GRP):
            value = jnp.dot(left_t[rows_half, q], right_m[s], preferred_element_type=F32)
            first = (2 * q + rows_half) * Z
            tri_src[1, s, pl.ds(first, Z)] = value.reshape(Z, ROWS, HALF).astype(BF16)

    def return_quadrant(rows_half, s):
        odd = lax.rem(plane + rows_half, 2)
        planes = [lax.rem(plane + (2 * a + odd), PLANES) * Z for a in (3, 2, 1, 0)]

        def one(other):
            remote(tri_src.at[1, s, other], tri_got.at[1, s, me], 9, tri_sem.at[1, s], dap=other).start()

        def step(p, carry):
            there = lax.rem(z + along(p), Z)
            for first in planes:
                one(first + there)
            return carry

        lax.fori_loop(0, Z - 1, step, 0)
        for first in planes[:3]:
            one(first + z)

        @pl.when(odd == 1)
        def _():
            one(planes[3] + z)

    def keep_own(s):
        own_triangle = own_copy(tri_src.at[1, s, me], tri_got.at[1, s, me], 6)
        own_triangle.start()
        own_triangle.wait()

    for k in range(GROUPS):
        wait_group(both_src, both_got, both_sem, 3, k)
        unpack(both_got, k * SLOTS, SLOTS, 0, unpacked, 0)
        share_turned(0, k)
        unpack(both_got, k * SLOTS, SLOTS, ROWS, right_m.at[0], k * BLOCK)
    received(left_t.at[0, pl.ds(0, GRP - 1)], turned_sem.at[0])
    quadrant(0, 0)
    return_quadrant(0, 0)
    for k in range(GROUPS):
        wait_group(late_src.at[0], late_got.at[0], late_left_sem, 4, k)
        unpack(late_got.at[0], k * SLOTS, SLOTS, 0, unpacked, 0)
        share_turned(1, k)
    received(left_t.at[1, pl.ds(0, GRP - 1)], turned_sem.at[1])
    quadrant(1, 0)
    return_quadrant(1, 0)
    keep_own(0)
    own_copy(late_src.at[1, me], late_got.at[1, DAP - 1], 5).wait()
    received(late_got.at[1, pl.ds(0, DAP - 1)], late_right_sem)
    unpack(late_got.at[1], 0, DAP, 0, right_m.at[1], 0)
    for rows_half in range(2):
        quadrant(rows_half, 1)
        return_quadrant(rows_half, 1)
    keep_own(1)
    finish(1, 0, True)
    finish(1, 1, True)

    most = pl.ds(0, DAP - 1)
    sent(right_src.at[most], 0)
    sent(left_src.at[most], 1)
    sent(right_mates.at[pl.ds(0, GRP - 1)], 3)
    sent(left_all.at[:, pl.ds(0, GRP - 1)], 4)
    sent(both_src.at[most], 5)
    sent(late_src.at[0, most], 6)
    sent(late_src.at[1, most], 7)
    sent(left_t.at[:, pl.ds(0, GRP - 1)], 8)
    sent(tri_src.at[0, :, most], 2)
    sent(tri_src.at[1, :, most], 9)


def shards(pair_rep, chain_ids, crop_lengths, ln_in_gain, w_proj, w_gate, ln_out_gain, w_out):
    hbm = pl.BlockSpec(memory_space=pltpu.HBM)
    vmem = pl.BlockSpec(memory_space=pltpu.VMEM)
    chain_tile = chain_ids.reshape(8, 128)
    wide, narrow = (DAP, 2 * ROWS, 128), (DAP, ROWS, 128)
    turned = (2, ROWS, CHAN, HALF)
    weight = (2, CHAN, CHAN)
    square = (BLOCK, COLS)
    dma = pltpu.SemaphoreType.DMA
    return pl.pallas_call(
        kernel,
        out_shape=jax.ShapeDtypeStruct(pair_rep.shape, BF16),
        in_specs=[hbm, hbm, pl.BlockSpec(memory_space=pltpu.SMEM)] + [hbm] * 5,
        out_specs=vmem,
        scratch_shapes=[
            *(
                pltpu.VMEM(x.shape, x.dtype)
                for x in (pair_rep, chain_tile, ln_in_gain, w_proj, w_gate, ln_out_gain, w_out)
            ),
            pltpu.VMEM((8, 1, 128), F32),
            pltpu.VMEM((2, ROWS, 1, HALF), F32),
            pltpu.VMEM(weight, F32),
            pltpu.VMEM(weight, F32),
            pltpu.VMEM((2, 2, 2 * CHAN, CHAN), BF16),
            pltpu.VMEM(weight, BF16),
            pltpu.VMEM(weight, BF16),
            pltpu.VMEM(turned, BF16),
            pltpu.VMEM(turned, BF16),
            pltpu.VMEM(turned, F32),
            pltpu.VMEM((CHAN * 2 * ROWS + 2 * ROWS, 128), F32),
            pltpu.VMEM((CHAN * ROWS + ROWS, 128), F32),
            pltpu.VMEM(wide, BF16),
            pltpu.VMEM(wide, BF16),
            pltpu.VMEM(wide, BF16),
            pltpu.VMEM(wide, BF16),
            pltpu.VMEM((GRP,) + square, BF16),
            pltpu.VMEM((GRP,) + square, BF16),
            pltpu.VMEM((GROUPS, GRP) + square, BF16),
            pltpu.VMEM((2, 2) + narrow, BF16),
            pltpu.VMEM((2, 2) + narrow, BF16),
            pltpu.VMEM(wide, BF16),
            pltpu.VMEM(wide, BF16),
            pltpu.VMEM((2,) + narrow, BF16),
            pltpu.VMEM((2,) + narrow, BF16),
            pltpu.VMEM((BLOCK, HALF), BF16),
            pltpu.VMEM((2, GRP, HALF, DAP * ROWS), BF16),
            pltpu.VMEM((2, DAP * ROWS, HALF), BF16),
            dma((7,)),
            dma((7,)),
            dma((10,)),
            dma,
            dma((GROUPS,)),
            dma,
            dma((GROUPS,)),
            dma((2, 2)),
            dma((GROUPS,)),
            dma((GROUPS,)),
            dma,
            dma((2,)),
        ],
        compiler_params=pltpu.CompilerParams(
            collective_id=0, has_side_effects=True, vmem_limit_bytes=63 << 20
        ),
        name="triangles",
    )(pair_rep, chain_tile, crop_lengths, ln_in_gain, w_proj, w_gate, ln_out_gain, w_out)


def solution(mesh):
    placed = (P("dap", "grp", None), P(), P(), P(), P(), P(), P(), P())
    return jax.shard_map(
        shards, mesh=mesh, in_specs=placed, out_specs=P("dap", "grp", None), check_vma=False
    )
```
